32 devices in a mesh: vessel: 4 (over z), tissue: 8 (over y, x, core).
Axes of the slice: x: 2, y: 2, z: 4, core: 2. Of those that a mesh axis runs over, the one named last changes fastest.
Arguments:
- tissue_start: float32 [3, 16, 64, 128], P(None, 'vessel', 'tissue'), may hold values from 0 to 1
- consumption: float32 [3, 16, 64, 128], P(None, 'vessel', 'tissue'), may hold values from 0.002 to 0.05
- inlet: float32 [3, 128], P(None, ('vessel', 'tissue')), may hold values from 0.5 to 2
- flow: float32 [128, 256], P(('vessel', 'tissue')), may hold values from 0.3 to 30
- permeability: float32 [3], replicated, may hold values from 0.3 to 3
- intersection_count: int32 [128, 8], P(('vessel', 'tissue')), may hold values from 64 to 128, as said below
- intersection_segment: int32 [128, 8, 128], P(('vessel', 'tissue')), may hold values from 0 to 255
- intersection_voxel: int32 [128, 8, 128], P(('vessel', 'tissue')), may hold values from 0 to 4095
- intersection_weight: float32 [128, 8, 128], P(('vessel', 'tissue')), may hold values from 0.1 to 1
- upstream: int32 [128], P(('vessel', 'tissue')), may hold values from 0 to 127
Outputs:
- tissue_field: float32 [3, 16, 64, 128], P(None, 'vessel', 'tissue')
- vessel_field: float32 [3, 128, 256], P(None, ('vessel', 'tissue'))
The draws below stay inside these ranges and needn't reach their ends.
Inputs may be any that keep to these rules, and one draw needn't show every extreme that they name: `intersection_count`: every block has all 128 slots live toward at least one tissue brick of its vessel part, at most 128 toward any, and at least 64 toward every other.
All inputs are finite; a program needn't handle non-finite values.
Results may differ from the reference program's by a relative error of at most 0.0001.
Values sent between devices are 32-bit elements; how exact they have to be, the bound alone decides.
A program may use at most 128 MiB of HBM per device.

```python
import math
import jax
import jax.numpy as jnp
from jax import lax

SPECIES = 3
SEG = 256
CAP = 128
OUTER = 2
SWEEPS = 4
CZ = 4
CY = 8
NX = 128
BLK_DEV = 4
NZ = 16
NY = 64
VOX = 4096
BLOCKS = 128
N_TISSUE = 8


def draw_intersection_count(key, part):
    bricks = NY // CY
    home_brick = jax.random.randint(jax.random.fold_in(key, 11), (BLOCKS,), 0, bricks)
    others = jax.random.randint(jax.random.fold_in(key, 12), (BLOCKS, bricks), CAP // 2, CAP + 1)
    column = jnp.arange(bricks)[None, :]
    return jnp.where(column == home_brick[:, None], CAP, others).astype(jnp.int32)


def place_ends(drawn, stream_key, smallest, largest):
    longest = drawn.shape.index(max(drawn.shape))
    spots = []
    for shift in (0, 1):
        where = [jax.random.randint(jax.random.fold_in(stream_key, axis), (), 0, length) for axis, length in enumerate(drawn.shape)]
        where[longest] = (where[longest] + shift) % drawn.shape[longest]
        spots.append(tuple(where))
    return drawn.at[spots[0]].set(smallest).at[spots[1]].set(largest)


def block_levels(own_key, dims, shards, low, high):
    gain, own = 1.0, jax.random.fold_in(own_key, 6)
    for axis_at, blocks in shards:
        heights = jnp.exp(jax.random.uniform(jax.random.fold_in(own, axis_at), (blocks,), jnp.float32, low / len(shards), high / len(shards)))
        gain = gain * jnp.repeat(heights, dims[axis_at] // blocks).reshape([-1 if axis == axis_at else 1 for axis in range(len(dims))])
    return gain


def setup_inputs(seed: int = 0) -> dict:
    arg_keys = jax.random.split(jax.random.key(seed), 11)
    return {
        "tissue_start": jnp.clip(1.0 * jax.random.uniform(arg_keys[0], (SPECIES, NZ, NY, NX), jnp.float32) ** block_levels(arg_keys[0], (SPECIES, NZ, NY, NX), ((1, 4), (2, 8)), -0.2, 0.2), 0.0, 1.0),
        "consumption": jnp.clip(jnp.exp(math.log(0.05) - 3.218876 * jax.random.uniform(arg_keys[1], (SPECIES, NZ, NY, NX), jnp.float32) ** block_levels(arg_keys[1], (SPECIES, NZ, NY, NX), ((1, 4), (2, 8)), -0.2, 0.2)), 0.002, 0.05),
        "inlet": jnp.clip(0.5 + 1.5 * jax.random.uniform(arg_keys[2], (SPECIES, BLOCKS), jnp.float32) ** block_levels(arg_keys[2], (SPECIES, BLOCKS), ((1, 32),), -0.2, 0.2), 0.5, 2.0),
        "flow": jnp.clip(jnp.exp(math.log(30.0) - 4.6051701 * jax.random.uniform(arg_keys[3], (BLOCKS, SEG), jnp.float32) ** block_levels(arg_keys[3], (BLOCKS, SEG), ((0, 32),), -0.2, 0.2)), 0.3, 30.0),
        "permeability": jnp.clip(jnp.exp(jax.random.uniform(arg_keys[4], (SPECIES,), jnp.float32, math.log(0.3), math.log(3.0))), 0.3, 3.0),
        "intersection_count": draw_intersection_count(jax.random.fold_in(arg_keys[10], 71), 0),
        "intersection_segment": place_ends(jax.random.randint(arg_keys[6], (BLOCKS, NY // CY, CAP), 0, SEG), jax.random.fold_in(arg_keys[6], 1), 0, SEG - 1).astype(jnp.int32),
        "intersection_voxel": place_ends(jax.random.randint(arg_keys[7], (BLOCKS, NY // CY, CAP), 0, VOX), jax.random.fold_in(arg_keys[7], 1), 0, VOX - 1).astype(jnp.int32),
        "intersection_weight": jnp.clip(jnp.exp(math.log(1.0) - 2.3025851 * jax.random.uniform(arg_keys[8], (BLOCKS, NY // CY, CAP), jnp.float32) ** block_levels(arg_keys[8], (BLOCKS, NY // CY, CAP), ((0, 32),), -0.2, 0.2)), 0.1, 1.0),
        "upstream": place_ends(jax.random.randint(arg_keys[9], (BLOCKS,), 0, BLOCKS), jax.random.fold_in(arg_keys[9], 1), 0, BLOCKS - 1).astype(jnp.int32),
    }


DIFFUSION = (1.0, 0.7, 0.7)


def combine(earlier, later):
    return earlier[0] * later[0], later[0] * earlier[1] + later[1]


def relax_sweep(tissue, source, consumption):
    padded = jnp.pad(tissue, ((0, 0), (1, 1), (1, 1), (1, 1)))
    neighbours = padded[:, 2:, 1:-1, 1:-1] + padded[:, :-2, 1:-1, 1:-1]
    neighbours = neighbours + padded[:, 1:-1, 2:, 1:-1] + padded[:, 1:-1, :-2, 1:-1]
    neighbours = neighbours + padded[:, 1:-1, 1:-1, 2:] + padded[:, 1:-1, 1:-1, :-2]
    rates = jnp.array(DIFFUSION, jnp.float32)[:, None, None, None]
    produced = jnp.zeros_like(tissue).at[2].set(2.0 * consumption[1] * tissue[1])
    return (source + produced + rates * neighbours) / (6.0 * rates + consumption)


def reference(tissue_start, consumption, inlet, flow, permeability, intersection_count, intersection_segment, intersection_voxel, intersection_weight, upstream):
    live_slot = jnp.arange(CAP).astype(jnp.int32)[None, None, :] < intersection_count[:, :, None]
    weight = jnp.where(live_slot, intersection_weight, 0.0).reshape(-1)
    block_index = jnp.arange(BLOCKS).astype(jnp.int32)[:, None, None]
    vessel_part = block_index // (BLK_DEV * N_TISSUE)
    column = jnp.arange(N_TISSUE).astype(jnp.int32)[None, :, None]
    voxel = intersection_voxel
    depth_index = vessel_part * CZ + voxel // (CY * NX)
    row_index = column * CY + (voxel // NX) % CY
    cell_index = ((depth_index * NY + row_index) * NX + voxel % NX).reshape(-1).astype(jnp.int32)
    owner = (block_index * SEG + intersection_segment).reshape(-1).astype(jnp.int32)
    weight_sum = jax.ops.segment_sum(weight, owner, BLOCKS * SEG).reshape(BLOCKS, SEG)
    tissue = tissue_start
    inflow = inlet
    vessel = jnp.zeros((SPECIES, BLOCKS, SEG), jnp.float32)
    for outer_step in range(OUTER):
        flat_field = tissue.reshape(SPECIES, -1)
        slot_values = flat_field[:, cell_index]
        gathered = jax.vmap(lambda species_row: jax.ops.segment_sum(species_row, owner, BLOCKS * SEG))(slot_values * weight[None, :])
        gathered = gathered.reshape(SPECIES, BLOCKS, SEG)
        denominator = flow[None] + permeability[:, None, None] * weight_sum[None]
        decay_rate = flow[None] / denominator
        drive_term = permeability[:, None, None] * gathered / denominator
        drive_term = drive_term.at[:, :, 0].add(decay_rate[:, :, 0] * inflow)
        _, vessel = lax.associative_scan(combine, (decay_rate, drive_term), axis=2)
        at_slot = vessel.reshape(SPECIES, -1)[:, owner]
        slot_flux = permeability[:, None] * weight[None, :] * (at_slot - slot_values)
        source = jax.vmap(lambda species_row: jax.ops.segment_sum(species_row, cell_index, NZ * NY * NX))(slot_flux)
        source = source.reshape(SPECIES, NZ, NY, NX)
        last_values = vessel[:, :, SEG - 1]
        inflow = 0.5 * (inlet + last_values[:, upstream])
        for sweep_step in range(SWEEPS):
            tissue = relax_sweep(tissue, source, consumption)
    return tissue, vessel
```

```python
import functools

import jax
import jax.numpy as jnp
from jax import lax
from jax.experimental import pallas as pl
from jax.experimental.pallas import tpu as pltpu
from jax.sharding import PartitionSpec as P

OUTER = 2
SWEEPS = 4
DIFFUSION = (1.0, 0.7, 0.7)
MESH = pl.DeviceIdType.MESH
F32 = jnp.float32
BF16 = jnp.bfloat16
LANES = 128

DIRS = ((1, 0), (-1, 0), (0, -1), (0, 1), (1, -1), (1, 1), (-1, -1), (-1, 1))
TISSUE, CONS, SOURCE = 0, 1, 2


def split_rows(x):
    high = x.astype(BF16).astype(F32)
    return jnp.concatenate([high, x - high], axis=0).astype(BF16)


def nt_dot(a, b):
    return lax.dot_general(a, b, (((1,), (1,)), ((), ())), preferred_element_type=F32)


def iota(shape, dim):
    return lax.broadcasted_iota(jnp.int32, shape, dim)


def kernel(
    n_v, n_t,
    tissue_ref, cons_ref, inlet_ref, flow_ref, perm_ref, count_ref, seg_ref, vox_ref, weight_ref, up_ref,
    tissue_out, vessel_out,
    send_vox, recv_vox, ohv, ohs, tsplit, acc,
    send_val, recv_val, send_flux, recv_flux,
    wrow, hrow, ends_own, ends_all,
    own, pack, halo_o, halo_p, field_a, field_b, ext_s, ext_i, ext_c,
    vox_ss, vox_rs, val_ss, val_rs, flux_ss, flux_rs, end_ss, end_rs, halo_ss, halo_rs,
):
    v, t = lax.axis_index("vessel"), lax.axis_index("tissue")
    species, cz, cy, nx = tissue_ref.shape
    blocks, _, slots = seg_ref.shape
    wide = n_t * slots
    rows = cz * cy
    kp = species + 1
    half = cy // 2

    def peer(d):
        return lax.rem(t + d, n_t)

    def vpeer(d):
        return lax.rem(v + d, n_v)

    def a2a(send, recv, ss, rs, d):
        return pltpu.make_async_remote_copy(
            src_ref=send.at[peer(d)], dst_ref=recv.at[t], send_sem=ss.at[d], recv_sem=rs.at[d],
            device_id={"tissue": peer(d)}, device_id_type=MESH)

    def ends_copy(d):
        per = n_t * blocks
        return pltpu.make_async_remote_copy(
            src_ref=ends_own, dst_ref=ends_all.at[pl.ds(v * per, per)], send_sem=end_ss.at[d], recv_sem=end_rs.at[d],
            device_id={"vessel": vpeer(d)}, device_id_type=MESH)

    def inside(dv, dt):
        return jnp.logical_and(
            jnp.logical_and(v + dv >= 0, v + dv < n_v), jnp.logical_and(t + dt >= 0, t + dt < n_t))

    barrier = pltpu.get_barrier_semaphore()
    for d in range(1, n_t):
        pl.semaphore_signal(barrier, inc=1, device_id={"tissue": peer(d)}, device_id_type=MESH)
    for d in range(1, n_v):
        pl.semaphore_signal(barrier, inc=1, device_id={"vessel": vpeer(d)}, device_id_type=MESH)
    greeted = jnp.int32(n_t - 1 + n_v - 1)
    for dv, dt in DIRS[4:]:
        @pl.when(inside(dv, dt))
        def _():
            pl.semaphore_signal(barrier, inc=1, device_id={"vessel": v + dv, "tissue": t + dt}, device_id_type=MESH)
        greeted = greeted + inside(dv, dt).astype(jnp.int32)

    for s in range(n_t):
        send_vox[s] = vox_ref[:, s, :]
    recv_vox[t] = send_vox[t]

    row8 = iota((cy, nx), 0)
    lane8 = iota((cy, nx), 1)
    low_half = row8 < half

    def put_own(which, ref):
        for z in range(cz):
            for k in range(species):
                own[which, z, k] = ref[k, z]

    def make_pack(which):
        for p in range(cz // 2):
            for k in range(species):
                even, odd = own[which, 2 * p, k], own[which, 2 * p + 1, k]
                pack[which, 0, p, k] = jnp.where(low_half, even, pltpu.roll(odd, half, 0))
                pack[which, 1, p, k] = jnp.where(low_half, pltpu.roll(even, half, 0), odd)

    def halo_copy(which, j):
        dv, dt = DIRS[j]
        whole = which in (TISSUE, 3)
        if dt == 0:
            cut = pl.ds(0, cz) if whole else (pl.ds(1, cz - 1) if dv > 0 else pl.ds(0, cz - 1))
            src, dst = own.at[which, cut], halo_o.at[which, j, cut]
        else:
            pairs = cz // 2
            cut = pl.ds(0, pairs) if whole or dv == 0 else (pl.ds(pairs - 1, 1) if dv > 0 else pl.ds(0, 1))
            src, dst = pack.at[which, 0 if dt < 0 else 1, cut], halo_p.at[which, j - 2, cut]
        return pltpu.make_async_remote_copy(
            src_ref=src, dst_ref=dst, send_sem=halo_ss.at[which, j], recv_sem=halo_rs.at[which, j],
            device_id={"vessel": v + dv, "tissue": t + dt}, device_id_type=MESH)

    def halo_send(which):
        for j, (dv, dt) in enumerate(DIRS):
            @pl.when(inside(dv, dt))
            def _():
                halo_copy(which, j).start()

    def halo_recv(which):
        for j, (dv, dt) in enumerate(DIRS):
            @pl.when(inside(-dv, -dt))
            def _():
                halo_copy(which, j).wait_recv()

    def halo_done(which):
        for j, (dv, dt) in enumerate(DIRS):
            @pl.when(inside(dv, dt))
            def _():
                halo_copy(which, j).wait_send()

    def extended(which, group, z, k):
        if group == 0:
            o = own[which, z, k]
        else:
            o = jnp.where(inside(-group, 0), halo_o[which, DIRS.index((group, 0)), z, k], 0.0)
        after = halo_p[which, DIRS.index((group, -1)) - 2, z // 2, k]
        before = halo_p[which, DIRS.index((group, 1)) - 2, z // 2, k]
        after = jnp.where(inside(-group, 1), after, 0.0)
        before = jnp.where(inside(-group, -1), before, 0.0)
        if z % 2 == 0:
            before = pltpu.roll(before, half, 0)
        else:
            after = pltpu.roll(after, half, 0)
        return o, jnp.where(low_half, after, before)

    put_own(TISSUE, tissue_ref)
    put_own(CONS, cons_ref)
    make_pack(TISSUE)
    make_pack(CONS)

    pl.semaphore_wait(barrier, greeted)

    for d in range(1, n_t):
        a2a(send_vox, recv_vox, vox_ss, vox_rs, d).start()

    lane_row = iota((1, slots), 1)
    lo_iota = iota((LANES, slots), 0)
    for b in range(blocks):
        for s in range(n_t):
            at = slice(s * slots, (s + 1) * slots)
            seg = seg_ref[b, s:s + 1, :]
            wrow[b, :, at] = jnp.where(lane_row < count_ref[b, s], weight_ref[b, s:s + 1, :], 0.0)
            hrow[b, :, at] = jnp.right_shift(seg, 7).astype(F32)
            lo = jnp.bitwise_and(seg, LANES - 1)
            ohs[b, :, at] = jnp.where(lo_iota == lo, 1.0, 0.0).astype(BF16)

    hi_iota = iota((rows, slots), 0)

    def build_cells(s):
        lo = jnp.bitwise_and(recv_vox[s], LANES - 1)
        for b in range(blocks):
            ohv[s, :, b * slots:(b + 1) * slots] = jnp.where(lo_iota == lo[b:b + 1], 1.0, 0.0).astype(BF16)

    def gather(s, dst, at):
        found = jnp.dot(tsplit[...], ohv[s], preferred_element_type=F32)
        hi = jnp.right_shift(recv_vox[s], 7)
        for b in range(blocks):
            mask = hi_iota == hi[b:b + 1]
            cut = slice(b * slots, (b + 1) * slots)
            for k in range(species):
                x = found[k * rows:(k + 1) * rows, cut] + found[(species + k) * rows:(species + k + 1) * rows, cut]
                dst[at, b * kp + k:b * kp + k + 1, :] = jnp.sum(jnp.where(mask, x, 0.0), axis=0, keepdims=True)
            dst[at, b * kp + species:(b + 1) * kp, :] = jnp.ones((1, slots), F32)

    def scatter(s, flux):
        hi = jnp.right_shift(recv_vox[s], 7)
        f = flux[s]
        parts = []
        for b in range(blocks):
            mask = hi_iota == hi[b:b + 1]
            parts.append(jnp.concatenate(
                [jnp.where(mask, f[b * kp + k:b * kp + k + 1], 0.0) for k in range(species)], axis=0))
        acc[...] += nt_dot(split_rows(jnp.concatenate(parts, axis=1)), ohv[s])

    def column(shape, per, values):
        at = lax.rem(iota(shape, 0), per)
        out = jnp.zeros(shape, F32)
        for r, x in values:
            out = jnp.where(at == r, x, out)
        return out

    n8 = 2 * kp
    vrows = blocks * n8
    vlane = iota((vrows, LANES), 1)
    vrow = iota((vrows, LANES), 0)
    first_half = lax.rem(vrow, n8) < kp
    perm_rows = column((vrows, LANES), kp, [(k, perm_ref[k]) for k in range(species)])
    perm4 = column((kp, LANES), kp, [(k, perm_ref[k]) for k in range(species)])[:, :1]
    inlet_rows = column(
        (vrows, LANES), vrows, [(b * n8 + k, inlet_ref[k, b]) for b in range(blocks) for k in range(species)])
    flow_rows = jnp.concatenate(
        [jnp.where(iota((n8, LANES), 0) < kp, flow_ref[b:b + 1, :LANES], flow_ref[b:b + 1, LANES:])
         for b in range(blocks)], axis=0)
    kp_row = iota((kp, slots), 0)

    def block_step(it):
        gathered, sums = [], []
        for b in range(blocks):
            x = jnp.concatenate([recv_val[it, s, b * kp:(b + 1) * kp, :] for s in range(n_t)], axis=1) * wrow[b]
            h = hrow[b]
            g = nt_dot(split_rows(jnp.concatenate([x * (1.0 - h), x * h], axis=0)), ohs[b])
            g = g[:n8] + g[n8:]
            gathered.append(g)
            sums.append(jnp.where(iota((n8, LANES), 0) < kp, g[species:kp], g[kp + species:n8]))
        gathered, sums = jnp.concatenate(gathered, axis=0), jnp.concatenate(sums, axis=0)
        denominator = flow_rows + perm_rows * sums
        a = flow_rows / denominator
        r = perm_rows * gathered / denominator
        step = 1
        while step < LANES:
            keep = vlane >= step
            a_before = jnp.where(keep, pltpu.roll(a, step, 1), 1.0)
            r_before = jnp.where(keep, pltpu.roll(r, step, 1), 0.0)
            r = a * r_before + r
            a = a * a_before
            step *= 2
        if it == 0:
            inflow = inlet_rows
        else:
            for d in range(1, n_v):
                ends_copy(d).wait_recv()
            fed = []
            for b in range(blocks):
                e = ends_all[up_ref[b]]
                pick = iota((n8, LANES), 0) == iota((n8, LANES), 1)
                pick = jnp.logical_and(pick, iota((n8, LANES), 0) < species)
                got = jnp.sum(jnp.where(pick, e, 0.0), axis=1, keepdims=True)
                fed.append(jnp.broadcast_to(got, (n8, LANES)))
            inflow = 0.5 * (inlet_rows + jnp.concatenate(fed, axis=0))
        first = r + a * inflow
        carried = jnp.broadcast_to(first[:, LANES - 1:], (vrows, LANES))
        field = r + a * jnp.where(first_half, inflow, pltpu.roll(carried, kp, 0))
        if it == OUTER - 1:
            for b in range(blocks):
                for k in range(species):
                    at = b * n8 + k
                    vessel_out[k, b:b + 1, :LANES] = field[at:at + 1]
                    vessel_out[k, b:b + 1, LANES:] = field[at + kp:at + kp + 1]
        last = jnp.broadcast_to(field[:, LANES - 1:], (vrows, LANES))
        for b in range(blocks):
            end = jnp.where(vrow - (b * n8 + kp) == vlane, last, 0.0)
            end = jnp.sum(jnp.where(vlane < species, end, 0.0), axis=0, keepdims=True)
            seen = jnp.dot(split_rows(field[b * n8:(b + 1) * n8]), ohs[b], preferred_element_type=F32)
            seen = seen[:n8] + seen[n8:]
            seen = jnp.where(hrow[b] > 0.5, seen[kp:], seen[:kp])
            x = jnp.concatenate([recv_val[it, s, b * kp:(b + 1) * kp, :] for s in range(n_t)], axis=1)
            flux = perm4 * wrow[b] * (seen - x)
            for s in range(n_t):
                send_flux[it, s, b * kp:(b + 1) * kp, :] = jnp.where(
                    kp_row == species, end, flux[:, s * slots:(s + 1) * slots])
        recv_flux[it, t] = send_flux[it, t]

    def sweep(src, dst, low, high, last):
        row_first, row_last = row8 == 0, row8 == cy - 1

        def slab(z, _):
            o = [src[0, z, k] for k in range(species)]
            h = [src[1, z, k] for k in range(species)]
            for k in range(species):
                back = [pltpu.roll(o[k], 1, 0), pltpu.roll(h[k], 1, 0)]
                fore = [pltpu.roll(o[k], cy - 1, 0), pltpu.roll(h[k], cy - 1, 0)]
                for part in range(1 if last else 2):
                    c = (o, h)[part][k]
                    nb = src[part, z - 1, k] + src[part, z + 1, k]
                    nb = nb + jnp.where(row_first, back[1 - part], back[part])
                    nb = nb + jnp.where(row_last, fore[1 - part], fore[part])
                    nb = nb + jnp.where(lane8 == 0, 0.0, pltpu.roll(c, 1, 1))
                    nb = nb + jnp.where(lane8 == nx - 1, 0.0, pltpu.roll(c, nx - 1, 1))
                    x = ext_s[part, z, k] + DIFFUSION[k] * nb
                    if k == 2:
                        x = x + ext_c[part, z] * (o, h)[part][1]
                    dst[part, z, k] = x * ext_i[part, z, k]
            return 0

        lax.fori_loop(low, high, slab, 0)

    def fill(which, ref):
        for g, group in enumerate((1, 0, -1)):
            for z in range(cz):
                for k in range(species):
                    o, h = extended(which, group, z, k)
                    ref[0, g * cz + z, k] = o
                    ref[1, g * cz + z, k] = h

    for it in range(OUTER):
        t_set, s_set = (TISSUE, SOURCE) if it == 0 else (3, 4)
        tsplit[...] = split_rows(jnp.concatenate(
            [own[t_set, z, k] for k in range(species) for z in range(cz)], axis=0))
        if it == 0:
            build_cells(t)

            def arrive(d, _):
                a2a(send_vox, recv_vox, vox_ss, vox_rs, d).wait_recv()
                s = lax.rem(t - d + n_t, n_t)
                build_cells(s)
                gather(s, send_val.at[it], s)
                a2a(send_val.at[it], recv_val.at[it], val_ss.at[it], val_rs.at[it], n_t - d).start()
                return 0
        else:
            def arrive(d, _):
                s = lax.rem(t - d + n_t, n_t)
                gather(s, send_val.at[it], s)
                a2a(send_val.at[it], recv_val.at[it], val_ss.at[it], val_rs.at[it], n_t - d).start()
                return 0
        lax.fori_loop(1, n_t, arrive, 0)
        gather(t, recv_val.at[it], t)
        halo_send(t_set)
        if it == 0:
            halo_send(CONS)
        for d in range(1, n_t):
            a2a(send_val.at[it], recv_val.at[it], val_ss.at[it], val_rs.at[it], d).wait_recv()
        block_step(it)
        for d in range(1, n_t):
            a2a(send_flux.at[it], recv_flux.at[it], flux_ss.at[it], flux_rs.at[it], d).start()
        acc[...] = jnp.zeros_like(acc)
        scatter(t, recv_flux.at[it])
        halo_recv(t_set)
        fill(t_set, field_a)
        if it == 0:
            halo_recv(CONS)
            for g, group in enumerate((1, 0, -1)):
                for z in range(cz):
                    for k in range(species):
                        parts = extended(CONS, group, z, k)
                        here = inside(-group, 0)
                        beside = jnp.where(
                            low_half,
                            jnp.where(inside(-group, 1), 1.0, 0.0), jnp.where(inside(-group, -1), 1.0, 0.0))
                        exists = (jnp.where(here, 1.0, 0.0), beside)
                        for part in range(2):
                            ext_i[part, g * cz + z, k] = exists[part] / (6.0 * DIFFUSION[k] + parts[part])
                            if k == 1:
                                ext_c[part, g * cz + z] = 2.0 * parts[part]

        def arrive_flux(d, _):
            a2a(send_flux.at[it], recv_flux.at[it], flux_ss.at[it], flux_rs.at[it], d).wait_recv()
            scatter(lax.rem(t - d + n_t, n_t), recv_flux.at[it])
            return 0
        lax.fori_loop(1, n_t, arrive_flux, 0)
        for k in range(species):
            for z in range(cz):
                at = k * rows + z * cy
                own[s_set, z, k] = acc[at:at + cy] + acc[species * rows + at:species * rows + at + cy]
        make_pack(s_set)
        halo_send(s_set)
        if it < OUTER - 1:
            for s in range(n_t):
                for b in range(blocks):
                    e = recv_flux[it, s, b * kp + species:(b + 1) * kp, :]
                    ends_own[s * blocks + b] = e
                    ends_all[(v * n_t + s) * blocks + b] = e
            for d in range(1, n_v):
                ends_copy(d).start()
        halo_recv(s_set)
        fill(s_set, ext_s)
        fields = (field_a, field_b)
        for n in range(SWEEPS):
            sweep(fields[n % 2], fields[(n + 1) % 2], n + 1, 3 * cz - 1 - n, n == SWEEPS - 1)
        final = fields[SWEEPS % 2]
        if it < OUTER - 1:
            for z in range(cz):
                for k in range(species):
                    own[3, z, k] = final[0, cz + z, k]
            make_pack(3)
        else:
            for z in range(cz):
                for k in range(species):
                    tissue_out[k, z] = final[0, cz + z, k]

    for d in range(1, n_t):
        a2a(send_vox, recv_vox, vox_ss, vox_rs, d).wait_send()
        for it in range(OUTER):
            a2a(send_val.at[it], recv_val.at[it], val_ss.at[it], val_rs.at[it], d).wait_send()
            a2a(send_flux.at[it], recv_flux.at[it], flux_ss.at[it], flux_rs.at[it], d).wait_send()
    for d in range(1, n_v):
        ends_copy(d).wait_send()
    for which in range(5):
        halo_done(which)


def solution(mesh):
    n_v, n_t = mesh.shape["vessel"], mesh.shape["tissue"]

    def shards(tissue, cons, inlet, flow, perm, count, seg, vox, weight, up):
        species, cz, cy, nx = tissue.shape
        blocks, _, slots = seg.shape
        kp, rows, pairs = species + 1, cz * cy, cz // 2
        vmem = pl.BlockSpec(memory_space=pltpu.VMEM)
        smem = pl.BlockSpec(memory_space=pltpu.SMEM)
        dma = pltpu.SemaphoreType.DMA
        tile = (species, cy, nx)
        message = pltpu.VMEM((OUTER, n_t, blocks * kp, slots), F32)
        ext = pltpu.VMEM((2, 3 * cz) + tile, F32)
        return pl.pallas_call(
            functools.partial(kernel, n_v, n_t),
            out_shape=(
                jax.ShapeDtypeStruct(tissue.shape, F32),
                jax.ShapeDtypeStruct((species, blocks, flow.shape[1]), F32),
            ),
            in_specs=[vmem, vmem, smem, vmem, smem, smem, vmem, vmem, vmem, smem],
            out_specs=(vmem, vmem),
            scratch_shapes=[
                pltpu.VMEM((n_t, blocks, slots), jnp.int32),
                pltpu.VMEM((n_t, blocks, slots), jnp.int32),
                pltpu.VMEM((n_t, LANES, blocks * slots), BF16),
                pltpu.VMEM((blocks, LANES, n_t * slots), BF16),
                pltpu.VMEM((2 * species * rows, nx), BF16),
                pltpu.VMEM((2 * species * rows, nx), F32),
                message, message, message, message,
                pltpu.VMEM((blocks, 1, n_t * slots), F32),
                pltpu.VMEM((blocks, 1, n_t * slots), F32),
                pltpu.VMEM((n_t * blocks, 1, slots), F32),
                pltpu.VMEM((n_v * n_t * blocks, 1, slots), F32),
                pltpu.VMEM((5, cz) + tile, F32),
                pltpu.VMEM((5, 2, pairs) + tile, F32),
                pltpu.VMEM((5, 2, cz) + tile, F32),
                pltpu.VMEM((5, 6, pairs) + tile, F32),
                ext, ext, ext, ext,
                pltpu.VMEM((2, 3 * cz, cy, nx), F32),
                dma((n_t,)), dma((n_t,)),
                dma((OUTER, n_t)), dma((OUTER, n_t)),
                dma((OUTER, n_t)), dma((OUTER, n_t)),
                dma((n_v,)), dma((n_v,)),
                dma((5, len(DIRS))), dma((5, len(DIRS))),
            ],
            compiler_params=pltpu.CompilerParams(collective_id=0, has_side_effects=True),
        )(tissue, cons, inlet, flow, perm, count, seg, vox, weight, up)

    both = ("vessel", "tissue")
    grid = P(None, "vessel", "tissue", None)
    return jax.shard_map(
        shards,
        mesh=mesh,
        in_specs=(
            grid, grid, P(None, both), P(both, None), P(), P(both, None),
            P(both, None, None), P(both, None, None), P(both, None, None), P(both),
        ),
        out_specs=(grid, P(None, both, None)),
        check_vma=False,
    )
```

```python
import functools

import jax
import jax.numpy as jnp
from jax import lax
from jax.experimental import pallas as pl
from jax.experimental.pallas import tpu as pltpu
from jax.sharding import PartitionSpec as P

OUTER = 2
SWEEPS = 4
DIFFUSION = (1.0, 0.7, 0.7)
MESH = pl.DeviceIdType.MESH
F32 = jnp.float32
BF16 = jnp.bfloat16
LANES = 128

DIRS = ((1, 0), (-1, 0), (0, -1), (0, 1), (1, -1), (1, 1), (-1, -1), (-1, 1))
TISSUE, CONS, SOURCE = 0, 1, 2


def split_rows(x):
    high = x.astype(BF16).astype(F32)
    return jnp.concatenate([high, x - high], axis=0).astype(BF16)


def nt_dot(a, b):
    return lax.dot_general(a, b, (((1,), (1,)), ((), ())), preferred_element_type=F32)


def iota(shape, dim):
    return lax.broadcasted_iota(jnp.int32, shape, dim)


def kernel(
    n_v, n_t,
    tissue_ref, cons_ref, inlet_ref, flow_ref, perm_ref, count_ref, seg_ref, vox_ref, weight_ref, up_ref,
    tissue_out, vessel_out,
    send_vox, recv_vox, ohv, ohs, tsplit, acc,
    send_val, recv_val, send_flux, recv_flux,
    wrow, hrow, coef, ends_own, ends_all,
    own, pack, halo_o, halo_p, field_a, field_b, ext_s, ext_i, ext_c,
    vox_ss, vox_rs, val_ss, val_rs, flux_ss, flux_rs, end_ss, end_rs, halo_ss, halo_rs,
):
    v, t = lax.axis_index("vessel"), lax.axis_index("tissue")
    species, cz, cy, nx = tissue_ref.shape
    blocks, _, slots = seg_ref.shape
    wide = n_t * slots
    rows = cz * cy
    kp = species + 1
    half = cy // 2

    def peer(d):
        return lax.rem(t + d, n_t)

    def vpeer(d):
        return lax.rem(v + d, n_v)

    def a2a(send, recv, ss, rs, d):
        return pltpu.make_async_remote_copy(
            src_ref=send.at[peer(d)], dst_ref=recv.at[t], send_sem=ss.at[d], recv_sem=rs.at[d],
            device_id={"tissue": peer(d)}, device_id_type=MESH)

    def ends_copy(d):
        per = n_t * blocks
        return pltpu.make_async_remote_copy(
            src_ref=ends_own, dst_ref=ends_all.at[pl.ds(v * per, per)], send_sem=end_ss.at[d], recv_sem=end_rs.at[d],
            device_id={"vessel": vpeer(d)}, device_id_type=MESH)

    def inside(dv, dt):
        return jnp.logical_and(
            jnp.logical_and(v + dv >= 0, v + dv < n_v), jnp.logical_and(t + dt >= 0, t + dt < n_t))

    barrier = pltpu.get_barrier_semaphore()
    for d in range(1, n_t):
        pl.semaphore_signal(barrier, inc=1, device_id={"tissue": peer(d)}, device_id_type=MESH)
    for d in range(1, n_v):
        pl.semaphore_signal(barrier, inc=1, device_id={"vessel": vpeer(d)}, device_id_type=MESH)
    greeted = jnp.int32(n_t - 1 + n_v - 1)
    for dv, dt in DIRS[4:]:
        @pl.when(inside(dv, dt))
        def _():
            pl.semaphore_signal(barrier, inc=1, device_id={"vessel": v + dv, "tissue": t + dt}, device_id_type=MESH)
        greeted = greeted + inside(dv, dt).astype(jnp.int32)

    for s in range(n_t):
        send_vox[s] = vox_ref[:, s, :]
    recv_vox[t] = send_vox[t]

    row8 = iota((cy, nx), 0)
    lane8 = iota((cy, nx), 1)
    low_half = row8 < half

    def put_own(which, ref):
        for z in range(cz):
            for k in range(species):
                own[which, z, k] = ref[k, z]

    def make_pack(which):
        for p in range(cz // 2):
            for k in range(species):
                even, odd = own[which, 2 * p, k], own[which, 2 * p + 1, k]
                pack[which, 0, p, k] = jnp.where(low_half, even, pltpu.roll(odd, half, 0))
                pack[which, 1, p, k] = jnp.where(low_half, pltpu.roll(even, half, 0), odd)

    def halo_copy(which, j):
        dv, dt = DIRS[j]
        whole = which in (TISSUE, 3)
        if dt == 0:
            cut = pl.ds(0, cz) if whole else (pl.ds(1, cz - 1) if dv > 0 else pl.ds(0, cz - 1))
            src, dst = own.at[which, cut], halo_o.at[which, j, cut]
        else:
            pairs = cz // 2
            cut = pl.ds(0, pairs) if whole or dv == 0 else (pl.ds(pairs - 1, 1) if dv > 0 else pl.ds(0, 1))
            src, dst = pack.at[which, 0 if dt < 0 else 1, cut], halo_p.at[which, j - 2, cut]
        return pltpu.make_async_remote_copy(
            src_ref=src, dst_ref=dst, send_sem=halo_ss.at[which, j], recv_sem=halo_rs.at[which, j],
            device_id={"vessel": v + dv, "tissue": t + dt}, device_id_type=MESH)

    def halo_send(which, chosen=range(len(DIRS))):
        for j in chosen:
            dv, dt = DIRS[j]

            @pl.when(inside(dv, dt))
            def _():
                halo_copy(which, j).start()

    def halo_recv(which):
        for j, (dv, dt) in enumerate(DIRS):
            @pl.when(inside(-dv, -dt))
            def _():
                halo_copy(which, j).wait_recv()

    def halo_done(which):
        for j, (dv, dt) in enumerate(DIRS):
            @pl.when(inside(dv, dt))
            def _():
                halo_copy(which, j).wait_send()

    def extended(which, group, z, k):
        if group == 0:
            o = own[which, z, k]
        else:
            o = jnp.where(inside(-group, 0), halo_o[which, DIRS.index((group, 0)), z, k], 0.0)
        after = halo_p[which, DIRS.index((group, -1)) - 2, z // 2, k]
        before = halo_p[which, DIRS.index((group, 1)) - 2, z // 2, k]
        after = jnp.where(inside(-group, 1), after, 0.0)
        before = jnp.where(inside(-group, -1), before, 0.0)
        if z % 2 == 0:
            before = pltpu.roll(before, half, 0)
        else:
            after = pltpu.roll(after, half, 0)
        return o, jnp.where(low_half, after, before)

    put_own(TISSUE, tissue_ref)
    put_own(CONS, cons_ref)
    make_pack(TISSUE)
    make_pack(CONS)

    lane_row = iota((1, slots), 1)
    lo_iota = iota((LANES, slots), 0)
    for b in range(blocks):
        for s in range(n_t):
            at = slice(s * slots, (s + 1) * slots)
            seg = seg_ref[b, s:s + 1, :]
            wrow[b, :, at] = jnp.where(lane_row < count_ref[b, s], weight_ref[b, s:s + 1, :], 0.0)
            hrow[b, :, at] = jnp.right_shift(seg, 7).astype(F32)
            lo = jnp.bitwise_and(seg, LANES - 1)
            ohs[b, :, at] = jnp.where(lo_iota == lo, 1.0, 0.0).astype(BF16)

    hi_iota = iota((rows, slots), 0)

    def build_cells(s):
        lo = jnp.bitwise_and(recv_vox[s], LANES - 1)
        for b in range(blocks):
            ohv[s, :, b * slots:(b + 1) * slots] = jnp.where(lo_iota == lo[b:b + 1], 1.0, 0.0).astype(BF16)

    def gather(s, dst, at):
        found = jnp.dot(tsplit[...], ohv[s], preferred_element_type=F32)
        hi = jnp.right_shift(recv_vox[s], 7)
        for b in range(blocks):
            mask = hi_iota == hi[b:b + 1]
            cut = slice(b * slots, (b + 1) * slots)
            for k in range(species):
                x = found[k * rows:(k + 1) * rows, cut] + found[(species + k) * rows:(species + k + 1) * rows, cut]
                dst[at, b * kp + k:b * kp + k + 1, :] = jnp.sum(jnp.where(mask, x, 0.0), axis=0, keepdims=True)
            dst[at, b * kp + species:(b + 1) * kp, :] = jnp.ones((1, slots), F32)

    def source_of(s, flux):
        hi = jnp.right_shift(recv_vox[s], 7)
        f = flux[s]
        parts = []
        for b in range(blocks):
            mask = hi_iota == hi[b:b + 1]
            parts.append(jnp.concatenate(
                [jnp.where(mask, f[b * kp + k:b * kp + k + 1], 0.0) for k in range(species)], axis=0))
        return nt_dot(split_rows(jnp.concatenate(parts, axis=1)), ohv[s])

    def column(shape, per, values):
        at = lax.rem(iota(shape, 0), per)
        out = jnp.zeros(shape, F32)
        for r, x in values:
            out = jnp.where(at == r, x, out)
        return out

    n8 = 2 * kp
    vrows = blocks * n8
    vlane = iota((vrows, LANES), 1)
    vrow = iota((vrows, LANES), 0)
    first_half = lax.rem(vrow, n8) < kp
    perm_rows = column((vrows, LANES), kp, [(k, perm_ref[k]) for k in range(species)])
    perm4 = column((kp, LANES), kp, [(k, perm_ref[k]) for k in range(species)])[:, :1]
    inlet_rows = column(
        (vrows, LANES), vrows, [(b * n8 + k, inlet_ref[k, b]) for b in range(blocks) for k in range(species)])
    flow_rows = jnp.concatenate(
        [jnp.where(iota((n8, LANES), 0) < kp, flow_ref[b:b + 1, :LANES], flow_ref[b:b + 1, LANES:])
         for b in range(blocks)], axis=0)
    kp_row = iota((kp, slots), 0)

    sums = []
    for b in range(blocks):
        h = hrow[b]
        x = jnp.where(iota((n8, wide), 0) < kp, wrow[b] * (1.0 - h), wrow[b] * h)
        g = nt_dot(split_rows(x), ohs[b])
        sums.append(g[:n8] + g[n8:])
    denominator = flow_rows + perm_rows * jnp.concatenate(sums, axis=0)
    a = flow_rows / denominator
    coef[8] = perm_rows / denominator
    steps = tuple(1 << n for n in range(LANES.bit_length() - 1))
    for n, step in enumerate(steps):
        keep = vlane >= step
        coef[n] = jnp.where(keep, a, 0.0)
        a = a * jnp.where(keep, pltpu.roll(a, step, 1), 1.0)
    coef[7] = a

    def block_step(it):
        gathered, values = [], []
        for b in range(blocks):
            x = jnp.concatenate([recv_val[it, s, b * kp:(b + 1) * kp, :] for s in range(n_t)], axis=1)
            values.append(x)
            x, h = x * wrow[b], hrow[b]
            g = nt_dot(split_rows(jnp.concatenate([x * (1.0 - h), x * h], axis=0)), ohs[b])
            gathered.append(g[:n8] + g[n8:])
        r = coef[8] * jnp.concatenate(gathered, axis=0)
        for n, step in enumerate(steps):
            r = r + coef[n] * pltpu.roll(r, step, 1)
        a = coef[7]
        if it == 0:
            inflow = inlet_rows
        else:
            for d in range(1, n_v):
                ends_copy(d).wait_recv()
            fed = []
            for b in range(blocks):
                e = ends_all[up_ref[b]]
                pick = iota((n8, LANES), 0) == iota((n8, LANES), 1)
                pick = jnp.logical_and(pick, iota((n8, LANES), 0) < species)
                got = jnp.sum(jnp.where(pick, e, 0.0), axis=1, keepdims=True)
                fed.append(jnp.broadcast_to(got, (n8, LANES)))
            inflow = 0.5 * (inlet_rows + jnp.concatenate(fed, axis=0))
        first = r + a * inflow
        carried = jnp.broadcast_to(first[:, LANES - 1:], (vrows, LANES))
        field = r + a * jnp.where(first_half, inflow, pltpu.roll(carried, kp, 0))
        if it == OUTER - 1:
            for b in range(blocks):
                for k in range(species):
                    at = b * n8 + k
                    vessel_out[k, b:b + 1, :LANES] = field[at:at + 1]
                    vessel_out[k, b:b + 1, LANES:] = field[at + kp:at + kp + 1]
        last = jnp.broadcast_to(field[:, LANES - 1:], (vrows, LANES))
        for b in range(blocks):
            end = jnp.where(vrow - (b * n8 + kp) == vlane, last, 0.0)
            end = jnp.sum(jnp.where(vlane < species, end, 0.0), axis=0, keepdims=True)
            seen = jnp.dot(split_rows(field[b * n8:(b + 1) * n8]), ohs[b], preferred_element_type=F32)
            seen = seen[:n8] + seen[n8:]
            seen = jnp.where(hrow[b] > 0.5, seen[kp:], seen[:kp])
            flux = perm4 * wrow[b] * (seen - values[b])
            for s in range(n_t):
                send_flux[it, s, b * kp:(b + 1) * kp, :] = jnp.where(
                    kp_row == species, end, flux[:, s * slots:(s + 1) * slots])
        recv_flux[it, t] = send_flux[it, t]

    def sweep(src, dst, low, high, last):
        row_first, row_last = row8 == 0, row8 == cy - 1

        seen = {}

        def tile(part, z, k):
            if (part, z, k) not in seen:
                seen[part, z, k] = src[part, z, k]
            return seen[part, z, k]

        for z in range(low, high):
            for k in range(species):
                both = (tile(0, z, k), tile(1, z, k))
                back = [pltpu.roll(c, 1, 0) for c in both]
                fore = [pltpu.roll(c, cy - 1, 0) for c in both]
                for part in range(1 if last else 2):
                    c = both[part]
                    nb = tile(part, z - 1, k) + tile(part, z + 1, k)
                    nb = nb + jnp.where(row_first, back[1 - part], back[part])
                    nb = nb + jnp.where(row_last, fore[1 - part], fore[part])
                    nb = nb + jnp.where(lane8 == 0, 0.0, pltpu.roll(c, 1, 1))
                    nb = nb + jnp.where(lane8 == nx - 1, 0.0, pltpu.roll(c, nx - 1, 1))
                    x = ext_s[part, z, k] + DIFFUSION[k] * nb
                    if k == 2:
                        x = x + ext_c[part, z] * tile(part, z, 1)
                    dst[part, z, k] = x * ext_i[part, z, k]

    def fill(which, ref):
        for g, group in enumerate((1, 0, -1)):
            for z in range(cz):
                for k in range(species):
                    o, h = extended(which, group, z, k)
                    ref[0, g * cz + z, k] = o
                    ref[1, g * cz + z, k] = h

    for it in range(OUTER):
        t_set, s_set = (TISSUE, SOURCE) if it == 0 else (3, 4)
        tsplit[...] = split_rows(jnp.concatenate(
            [own[t_set, z, k] for k in range(species) for z in range(cz)], axis=0))
        if it == 0:
            build_cells(t)
            gather(t, recv_val.at[it], t)
            pl.semaphore_wait(barrier, greeted)
            for d in range(1, n_t):
                a2a(send_vox, recv_vox, vox_ss, vox_rs, d).start()

            def arrive(d, _):
                a2a(send_vox, recv_vox, vox_ss, vox_rs, d).wait_recv()
                s = lax.rem(t - d + n_t, n_t)
                build_cells(s)
                gather(s, send_val.at[it], s)
                a2a(send_val.at[it], recv_val.at[it], val_ss.at[it], val_rs.at[it], n_t - d).start()
                return 0
        else:
            def arrive(d, _):
                s = lax.rem(t - d + n_t, n_t)
                gather(s, send_val.at[it], s)
                a2a(send_val.at[it], recv_val.at[it], val_ss.at[it], val_rs.at[it], n_t - d).start()
                return 0
        lax.fori_loop(1, n_t, arrive, 0)
        if it > 0:
            gather(t, recv_val.at[it], t)
        halo_send(t_set)
        if it == 0:
            halo_send(CONS)
        for d in range(1, n_t):
            a2a(send_val.at[it], recv_val.at[it], val_ss.at[it], val_rs.at[it], d).wait_recv()
        block_step(it)
        for d in range(1, n_t):
            a2a(send_flux.at[it], recv_flux.at[it], flux_ss.at[it], flux_rs.at[it], d).start()
        acc[...] = source_of(t, recv_flux.at[it])
        halo_recv(t_set)
        fill(t_set, field_a)
        if it == 0:
            halo_recv(CONS)
            for g, group in enumerate((1, 0, -1)):
                for z in range(cz):
                    for k in range(species):
                        parts = extended(CONS, group, z, k)
                        here = inside(-group, 0)
                        beside = jnp.where(
                            low_half,
                            jnp.where(inside(-group, 1), 1.0, 0.0), jnp.where(inside(-group, -1), 1.0, 0.0))
                        exists = (jnp.where(here, 1.0, 0.0), beside)
                        for part in range(2):
                            ext_i[part, g * cz + z, k] = exists[part] / (6.0 * DIFFUSION[k] + parts[part])
                            if k == 1:
                                ext_c[part, g * cz + z] = 2.0 * parts[part]

        for d in range(1, n_t):
            a2a(send_flux.at[it], recv_flux.at[it], flux_ss.at[it], flux_rs.at[it], d).wait_recv()
        total = acc[...]
        for d in range(1, n_t):
            total = total + source_of(lax.rem(t - d + n_t, n_t), recv_flux.at[it])
        for k in range(species):
            for z in range(cz):
                at = k * rows + z * cy
                both = total[at:at + cy] + total[species * rows + at:species * rows + at + cy]
                own[s_set, z, k] = both
                ext_s[0, cz + z, k] = both
        halo_send(s_set, (0, 1))
        make_pack(s_set)
        halo_send(s_set, range(2, len(DIRS)))
        if it < OUTER - 1:
            for s in range(n_t):
                for b in range(blocks):
                    e = recv_flux[it, s, b * kp + species:(b + 1) * kp, :]
                    ends_own[s * blocks + b] = e
                    ends_all[(v * n_t + s) * blocks + b] = e
            for d in range(1, n_v):
                ends_copy(d).start()
        halo_recv(s_set)
        fill(s_set, ext_s)
        fields = (field_a, field_b)
        for n in range(SWEEPS):
            sweep(fields[n % 2], fields[(n + 1) % 2], n + 1, 3 * cz - 1 - n, n == SWEEPS - 1)
        final = fields[SWEEPS % 2]
        if it < OUTER - 1:
            for z in range(cz):
                for k in range(species):
                    own[3, z, k] = final[0, cz + z, k]
            make_pack(3)
        else:
            for z in range(cz):
                for k in range(species):
                    tissue_out[k, z] = final[0, cz + z, k]

    for d in range(1, n_t):
        a2a(send_vox, recv_vox, vox_ss, vox_rs, d).wait_send()
        for it in range(OUTER):
            a2a(send_val.at[it], recv_val.at[it], val_ss.at[it], val_rs.at[it], d).wait_send()
            a2a(send_flux.at[it], recv_flux.at[it], flux_ss.at[it], flux_rs.at[it], d).wait_send()
    for d in range(1, n_v):
        ends_copy(d).wait_send()
    for which in range(5):
        halo_done(which)


def solution(mesh):
    n_v, n_t = mesh.shape["vessel"], mesh.shape["tissue"]

    def shards(tissue, cons, inlet, flow, perm, count, seg, vox, weight, up):
        species, cz, cy, nx = tissue.shape
        blocks, _, slots = seg.shape
        kp, rows, pairs = species + 1, cz * cy, cz // 2
        vmem = pl.BlockSpec(memory_space=pltpu.VMEM)
        smem = pl.BlockSpec(memory_space=pltpu.SMEM)
        dma = pltpu.SemaphoreType.DMA
        tile = (species, cy, nx)
        message = pltpu.VMEM((OUTER, n_t, blocks * kp, slots), F32)
        ext = pltpu.VMEM((2, 3 * cz) + tile, F32)
        return pl.pallas_call(
            functools.partial(kernel, n_v, n_t),
            out_shape=(
                jax.ShapeDtypeStruct(tissue.shape, F32),
                jax.ShapeDtypeStruct((species, blocks, flow.shape[1]), F32),
            ),
            in_specs=[vmem, vmem, smem, vmem, smem, smem, vmem, vmem, vmem, smem],
            out_specs=(vmem, vmem),
            scratch_shapes=[
                pltpu.VMEM((n_t, blocks, slots), jnp.int32),
                pltpu.VMEM((n_t, blocks, slots), jnp.int32),
                pltpu.VMEM((n_t, LANES, blocks * slots), BF16),
                pltpu.VMEM((blocks, LANES, n_t * slots), BF16),
                pltpu.VMEM((2 * species * rows, nx), BF16),
                pltpu.VMEM((2 * species * rows, nx), F32),
                message, message, message, message,
                pltpu.VMEM((blocks, 1, n_t * slots), F32),
                pltpu.VMEM((blocks, 1, n_t * slots), F32),
                pltpu.VMEM((9, blocks * 2 * kp, LANES), F32),
                pltpu.VMEM((n_t * blocks, 1, slots), F32),
                pltpu.VMEM((n_v * n_t * blocks, 1, slots), F32),
                pltpu.VMEM((5, cz) + tile, F32),
                pltpu.VMEM((5, 2, pairs) + tile, F32),
                pltpu.VMEM((5, 2, cz) + tile, F32),
                pltpu.VMEM((5, 6, pairs) + tile, F32),
                ext, ext, ext, ext,
                pltpu.VMEM((2, 3 * cz, cy, nx), F32),
                dma((n_t,)), dma((n_t,)),
                dma((OUTER, n_t)), dma((OUTER, n_t)),
                dma((OUTER, n_t)), dma((OUTER, n_t)),
                dma((n_v,)), dma((n_v,)),
                dma((5, len(DIRS))), dma((5, len(DIRS))),
            ],
            compiler_params=pltpu.CompilerParams(collective_id=0, has_side_effects=True),
        )(tissue, cons, inlet, flow, perm, count, seg, vox, weight, up)

    both = ("vessel", "tissue")
    grid = P(None, "vessel", "tissue", None)
    return jax.shard_map(
        shards,
        mesh=mesh,
        in_specs=(
            grid, grid, P(None, both), P(both, None), P(), P(both, None),
            P(both, None, None), P(both, None, None), P(both, None, None), P(both),
        ),
        out_specs=(grid, P(None, both, None)),
        check_vma=False,
    )
```

```python
import functools

import jax
import jax.numpy as jnp
from jax import lax
from jax.experimental import pallas as pl
from jax.experimental.pallas import tpu as pltpu
from jax.sharding import PartitionSpec as P

OUTER = 2
SWEEPS = 4
DIFFUSION = (1.0, 0.7, 0.7)
MESH = pl.DeviceIdType.MESH
F32 = jnp.float32
BF16 = jnp.bfloat16
LANES = 128

DIRS = ((1, 0), (-1, 0), (0, -1), (0, 1), (1, -1), (1, 1), (-1, -1), (-1, 1))
TISSUE, CONS, SOURCE = 0, 1, 2


def split_rows(x):
    high = x.astype(BF16).astype(F32)
    return jnp.concatenate([high, x - high], axis=0).astype(BF16)


def nt_dot(a, b):
    return lax.dot_general(a, b, (((1,), (1,)), ((), ())), preferred_element_type=F32)


def iota(shape, dim):
    return lax.broadcasted_iota(jnp.int32, shape, dim)


def kernel(
    n_v, n_t,
    tissue_in, cons_in, inlet_in, flow_in, perm_in, count_in, seg_in, vox_in, weight_in, up_in,
    tissue_out, vessel_out,
    tissue_ref, cons_ref, inlet_ref, flow_ref, perm_ref, count_ref, seg_ref, vox_ref, weight_ref, up_ref, in_sem,
    send_vox, recv_vox, ohv, ohs, tsplit, acc,
    send_val, recv_val, send_flux, recv_flux,
    wrow, hrow, coef, ends_own, ends_all,
    own, pack, halo_o, halo_p, field_a, field_b, ext_s, ext_i, ext_c,
    vox_ss, vox_rs, val_ss, val_rs, flux_ss, flux_rs, end_ss, end_rs, halo_ss, halo_rs,
):
    v, t = lax.axis_index("vessel"), lax.axis_index("tissue")
    species, cz, cy, nx = tissue_ref.shape
    blocks, _, slots = seg_ref.shape
    wide = n_t * slots
    rows = cz * cy
    kp = species + 1
    half = cy // 2

    pairwise = n_t & (n_t - 1) == 0

    def peer(d):
        if not pairwise:
            return lax.rem(t + d, n_t)
        other = t
        for bit in (1 << n for n in range(n_t.bit_length() - 1)):
            if d & bit:
                other = other + bit * (1 - 2 * lax.rem(lax.div(t, bit), 2))
        return other

    def sender(d):
        return peer(d) if pairwise else lax.rem(t - d + n_t, n_t)

    def back(d):
        return d if pairwise else n_t - d

    def vpeer(d):
        return lax.rem(v + d, n_v)

    def a2a(send, recv, ss, rs, d):
        return pltpu.make_async_remote_copy(
            src_ref=send.at[peer(d)], dst_ref=recv.at[t], send_sem=ss.at[d], recv_sem=rs.at[d],
            device_id={"tissue": peer(d)}, device_id_type=MESH)

    def ends_copy(d):
        per = n_t * blocks
        return pltpu.make_async_remote_copy(
            src_ref=ends_own, dst_ref=ends_all.at[pl.ds(v * per, per)], send_sem=end_ss.at[d], recv_sem=end_rs.at[d],
            device_id={"vessel": vpeer(d)}, device_id_type=MESH)

    def inside(dv, dt):
        return jnp.logical_and(
            jnp.logical_and(v + dv >= 0, v + dv < n_v), jnp.logical_and(t + dt >= 0, t + dt < n_t))

    barrier = pltpu.get_barrier_semaphore()
    for d in range(1, n_t):
        pl.semaphore_signal(barrier, inc=1, device_id={"tissue": peer(d)}, device_id_type=MESH)
    for d in range(1, n_v):
        pl.semaphore_signal(barrier, inc=1, device_id={"vessel": vpeer(d)}, device_id_type=MESH)
    greeted = jnp.int32(n_t - 1 + n_v - 1)
    for dv, dt in DIRS[4:]:
        @pl.when(inside(dv, dt))
        def _():
            pl.semaphore_signal(barrier, inc=1, device_id={"vessel": v + dv, "tissue": t + dt}, device_id_type=MESH)
        greeted = greeted + inside(dv, dt).astype(jnp.int32)

    places = (
        (vox_in, vox_ref), (tissue_in, tissue_ref), (seg_in, seg_ref), (count_in, count_ref), (weight_in, weight_ref),
        (cons_in, cons_ref), (perm_in, perm_ref), (flow_in, flow_ref), (inlet_in, inlet_ref), (up_in, up_ref))
    for n, (src, dst) in enumerate(places):
        pltpu.make_async_copy(src, dst, in_sem.at[n]).start()
    for n, (src, dst) in enumerate(places):
        pltpu.make_async_copy(src, dst, in_sem.at[n]).wait()
    for s in range(n_t):
        send_vox[s] = vox_ref[:, s, :]
    recv_vox[t] = send_vox[t]

    row8 = iota((cy, nx), 0)
    lane8 = iota((cy, nx), 1)
    low_half = row8 < half

    def put_own(which, ref):
        for z in range(cz):
            for k in range(species):
                own[which, z, k] = ref[k, z]

    def make_pack(which):
        for p in range(cz // 2):
            for k in range(species):
                even, odd = own[which, 2 * p, k], own[which, 2 * p + 1, k]
                pack[which, 0, p, k] = jnp.where(low_half, even, pltpu.roll(odd, half, 0))
                pack[which, 1, p, k] = jnp.where(low_half, pltpu.roll(even, half, 0), odd)

    def halo_copy(which, j):
        dv, dt = DIRS[j]
        whole = which in (TISSUE, 3)
        if dt == 0:
            cut = pl.ds(0, cz) if whole else (pl.ds(1, cz - 1) if dv > 0 else pl.ds(0, cz - 1))
            src, dst = own.at[which, cut], halo_o.at[which, j, cut]
        else:
            pairs = cz // 2
            cut = pl.ds(0, pairs) if whole or dv == 0 else (pl.ds(pairs - 1, 1) if dv > 0 else pl.ds(0, 1))
            src, dst = pack.at[which, 0 if dt < 0 else 1, cut], halo_p.at[which, j - 2, cut]
        return pltpu.make_async_remote_copy(
            src_ref=src, dst_ref=dst, send_sem=halo_ss.at[which, j], recv_sem=halo_rs.at[which, j],
            device_id={"vessel": v + dv, "tissue": t + dt}, device_id_type=MESH)

    def halo_send(which, chosen=range(len(DIRS))):
        for j in chosen:
            dv, dt = DIRS[j]

            @pl.when(inside(dv, dt))
            def _():
                halo_copy(which, j).start()

    def halo_recv(which):
        for j, (dv, dt) in enumerate(DIRS):
            @pl.when(inside(-dv, -dt))
            def _():
                halo_copy(which, j).wait_recv()

    def halo_done(which):
        for j, (dv, dt) in enumerate(DIRS):
            @pl.when(inside(dv, dt))
            def _():
                halo_copy(which, j).wait_send()

    def extended(which, group, z, k):
        if group == 0:
            o = own[which, z, k]
        else:
            o = jnp.where(inside(-group, 0), halo_o[which, DIRS.index((group, 0)), z, k], 0.0)
        after = halo_p[which, DIRS.index((group, -1)) - 2, z // 2, k]
        before = halo_p[which, DIRS.index((group, 1)) - 2, z // 2, k]
        after = jnp.where(inside(-group, 1), after, 0.0)
        before = jnp.where(inside(-group, -1), before, 0.0)
        if z % 2 == 0:
            before = pltpu.roll(before, half, 0)
        else:
            after = pltpu.roll(after, half, 0)
        return o, jnp.where(low_half, after, before)

    put_own(TISSUE, tissue_ref)
    put_own(CONS, cons_ref)
    make_pack(TISSUE)
    make_pack(CONS)

    lane_row = iota((1, slots), 1)
    lo_iota = iota((LANES, slots), 0)
    for b in range(blocks):
        for s in range(n_t):
            at = slice(s * slots, (s + 1) * slots)
            seg = seg_ref[b, s:s + 1, :]
            wrow[b, :, at] = jnp.where(lane_row < count_ref[b, s], weight_ref[b, s:s + 1, :], 0.0)
            hrow[b, :, at] = jnp.right_shift(seg, 7).astype(F32)
            lo = jnp.bitwise_and(seg, LANES - 1)
            ohs[b, :, at] = jnp.where(lo_iota == lo, 1.0, 0.0).astype(BF16)

    hi_iota = iota((rows, slots), 0)

    def build_cells(s):
        lo = jnp.bitwise_and(recv_vox[s], LANES - 1)
        for b in range(blocks):
            ohv[s, :, b * slots:(b + 1) * slots] = jnp.where(lo_iota == lo[b:b + 1], 1.0, 0.0).astype(BF16)

    def gather(s, dst, at):
        found = jnp.dot(tsplit[...], ohv[s], preferred_element_type=F32)
        hi = jnp.right_shift(recv_vox[s], 7)
        for b in range(blocks):
            mask = hi_iota == hi[b:b + 1]
            cut = slice(b * slots, (b + 1) * slots)
            for k in range(species):
                x = found[k * rows:(k + 1) * rows, cut] + found[(species + k) * rows:(species + k + 1) * rows, cut]
                dst[at, b * kp + k:b * kp + k + 1, :] = jnp.sum(jnp.where(mask, x, 0.0), axis=0, keepdims=True)
            dst[at, b * kp + species:(b + 1) * kp, :] = jnp.ones((1, slots), F32)

    def source_of(s, flux):
        hi = jnp.right_shift(recv_vox[s], 7)
        f = flux[s]
        parts = []
        for b in range(blocks):
            mask = hi_iota == hi[b:b + 1]
            parts.append(jnp.concatenate(
                [jnp.where(mask, f[b * kp + k:b * kp + k + 1], 0.0) for k in range(species)], axis=0))
        return nt_dot(split_rows(jnp.concatenate(parts, axis=1)), ohv[s])

    def column(shape, per, values):
        at = lax.rem(iota(shape, 0), per)
        out = jnp.zeros(shape, F32)
        for r, x in values:
            out = jnp.where(at == r, x, out)
        return out

    n8 = 2 * kp
    vrows = blocks * n8
    vlane = iota((vrows, LANES), 1)
    vrow = iota((vrows, LANES), 0)
    first_half = lax.rem(vrow, n8) < kp
    perm_rows = column((vrows, LANES), kp, [(k, perm_ref[k]) for k in range(species)])
    perm4 = column((kp, LANES), kp, [(k, perm_ref[k]) for k in range(species)])[:, :1]
    inlet_rows = column(
        (vrows, LANES), vrows, [(b * n8 + k, inlet_ref[k, b]) for b in range(blocks) for k in range(species)])
    flow_rows = jnp.concatenate(
        [jnp.where(iota((n8, LANES), 0) < kp, flow_ref[b:b + 1, :LANES], flow_ref[b:b + 1, LANES:])
         for b in range(blocks)], axis=0)
    kp_row = iota((kp, slots), 0)

    sums = []
    for b in range(blocks):
        h = hrow[b]
        x = jnp.where(iota((n8, wide), 0) < kp, wrow[b] * (1.0 - h), wrow[b] * h)
        g = nt_dot(split_rows(x), ohs[b])
        sums.append(g[:n8] + g[n8:])
    denominator = flow_rows + perm_rows * jnp.concatenate(sums, axis=0)
    a = flow_rows / denominator
    coef[8] = perm_rows / denominator
    steps = tuple(1 << n for n in range(LANES.bit_length() - 1))
    for n, step in enumerate(steps):
        keep = vlane >= step
        coef[n] = jnp.where(keep, a, 0.0)
        a = a * jnp.where(keep, pltpu.roll(a, step, 1), 1.0)
    coef[7] = a

    def block_step(it):
        gathered, values = [], []
        for b in range(blocks):
            x = jnp.concatenate([recv_val[it, s, b * kp:(b + 1) * kp, :] for s in range(n_t)], axis=1)
            values.append(x)
            x, h = x * wrow[b], hrow[b]
            g = nt_dot(split_rows(jnp.concatenate([x * (1.0 - h), x * h], axis=0)), ohs[b])
            gathered.append(g[:n8] + g[n8:])
        r = coef[8] * jnp.concatenate(gathered, axis=0)
        for n, step in enumerate(steps):
            r = r + coef[n] * pltpu.roll(r, step, 1)
        a = coef[7]
        if it == 0:
            inflow = inlet_rows
        else:
            for d in range(1, n_v):
                ends_copy(d).wait_recv()
            fed = []
            for b in range(blocks):
                e = ends_all[up_ref[b]]
                pick = iota((n8, LANES), 0) == iota((n8, LANES), 1)
                pick = jnp.logical_and(pick, iota((n8, LANES), 0) < species)
                got = jnp.sum(jnp.where(pick, e, 0.0), axis=1, keepdims=True)
                fed.append(jnp.broadcast_to(got, (n8, LANES)))
            inflow = 0.5 * (inlet_rows + jnp.concatenate(fed, axis=0))
        first = r + a * inflow
        carried = jnp.broadcast_to(first[:, LANES - 1:], (vrows, LANES))
        field = r + a * jnp.where(first_half, inflow, pltpu.roll(carried, kp, 0))
        if it == OUTER - 1:
            for b in range(blocks):
                for k in range(species):
                    at = b * n8 + k
                    vessel_out[k, b:b + 1, :LANES] = field[at:at + 1]
                    vessel_out[k, b:b + 1, LANES:] = field[at + kp:at + kp + 1]
        last = jnp.broadcast_to(field[:, LANES - 1:], (vrows, LANES))
        for b in range(blocks):
            end = jnp.where(vrow - (b * n8 + kp) == vlane, last, 0.0)
            end = jnp.sum(jnp.where(vlane < species, end, 0.0), axis=0, keepdims=True)
            seen = jnp.dot(split_rows(field[b * n8:(b + 1) * n8]), ohs[b], preferred_element_type=F32)
            seen = seen[:n8] + seen[n8:]
            seen = jnp.where(hrow[b] > 0.5, seen[kp:], seen[:kp])
            flux = perm4 * wrow[b] * (seen - values[b])
            for s in range(n_t):
                send_flux[it, s, b * kp:(b + 1) * kp, :] = jnp.where(
                    kp_row == species, end, flux[:, s * slots:(s + 1) * slots])
        recv_flux[it, t] = send_flux[it, t]

    def sweep(src, dst, low, high, last):
        row_first, row_last = row8 == 0, row8 == cy - 1

        seen = {}

        def tile(part, z, k):
            if (part, z, k) not in seen:
                seen[part, z, k] = src[part, z, k]
            return seen[part, z, k]

        for z in range(low, high):
            for k in range(species):
                both = (tile(0, z, k), tile(1, z, k))
                back = [pltpu.roll(c, 1, 0) for c in both]
                fore = [pltpu.roll(c, cy - 1, 0) for c in both]
                for part in range(1 if last else 2):
                    c = both[part]
                    nb = tile(part, z - 1, k) + tile(part, z + 1, k)
                    nb = nb + jnp.where(row_first, back[1 - part], back[part])
                    nb = nb + jnp.where(row_last, fore[1 - part], fore[part])
                    nb = nb + jnp.where(lane8 == 0, 0.0, pltpu.roll(c, 1, 1))
                    nb = nb + jnp.where(lane8 == nx - 1, 0.0, pltpu.roll(c, nx - 1, 1))
                    x = ext_s[part, z, k] + DIFFUSION[k] * nb
                    if k == 2:
                        x = x + ext_c[part, z] * tile(part, z, 1)
                    dst[part, z, k] = x * ext_i[part, z, k]

    def fill(which, ref):
        for g, group in enumerate((1, 0, -1)):
            for z in range(cz):
                for k in range(species):
                    o, h = extended(which, group, z, k)
                    ref[0, g * cz + z, k] = o
                    ref[1, g * cz + z, k] = h

    for it in range(OUTER):
        t_set, s_set = (TISSUE, SOURCE) if it == 0 else (3, 4)
        tsplit[...] = split_rows(jnp.concatenate(
            [own[t_set, z, k] for k in range(species) for z in range(cz)], axis=0))
        if it == 0:
            build_cells(t)
            gather(t, recv_val.at[it], t)
            pl.semaphore_wait(barrier, greeted)
            for d in reversed(range(1, n_t)):
                a2a(send_vox, recv_vox, vox_ss, vox_rs, d).start()

            for d in range(1, n_t):
                a2a(send_vox, recv_vox, vox_ss, vox_rs, d).wait_recv()
                build_cells(sender(d))
                gather(sender(d), send_val.at[it], sender(d))
                a2a(send_val.at[it], recv_val.at[it], val_ss.at[it], val_rs.at[it], back(d)).start()
        else:
            for d in reversed(range(1, n_t)):
                gather(peer(d), send_val.at[it], peer(d))
                a2a(send_val.at[it], recv_val.at[it], val_ss.at[it], val_rs.at[it], d).start()
        if it > 0:
            gather(t, recv_val.at[it], t)
        halo_send(t_set)
        if it == 0:
            halo_send(CONS)
        for d in range(1, n_t):
            a2a(send_val.at[it], recv_val.at[it], val_ss.at[it], val_rs.at[it], d).wait_recv()
        block_step(it)
        for d in reversed(range(1, n_t)):
            a2a(send_flux.at[it], recv_flux.at[it], flux_ss.at[it], flux_rs.at[it], d).start()
        acc[...] = source_of(t, recv_flux.at[it])
        halo_recv(t_set)
        fill(t_set, field_a)
        if it == 0:
            halo_recv(CONS)
            for g, group in enumerate((1, 0, -1)):
                for z in range(cz):
                    for k in range(species):
                        parts = extended(CONS, group, z, k)
                        here = inside(-group, 0)
                        beside = jnp.where(
                            low_half,
                            jnp.where(inside(-group, 1), 1.0, 0.0), jnp.where(inside(-group, -1), 1.0, 0.0))
                        exists = (jnp.where(here, 1.0, 0.0), beside)
                        for part in range(2):
                            ext_i[part, g * cz + z, k] = exists[part] / (6.0 * DIFFUSION[k] + parts[part])
                            if k == 1:
                                ext_c[part, g * cz + z] = 2.0 * parts[part]

        for d in range(1, n_t):
            a2a(send_flux.at[it], recv_flux.at[it], flux_ss.at[it], flux_rs.at[it], d).wait_recv()
        total = acc[...]
        for d in range(1, n_t):
            total = total + source_of(sender(d), recv_flux.at[it])
        for k in range(species):
            for z in range(cz):
                at = k * rows + z * cy
                both = total[at:at + cy] + total[species * rows + at:species * rows + at + cy]
                own[s_set, z, k] = both
                ext_s[0, cz + z, k] = both
        make_pack(s_set)
        halo_send(s_set, (4, 5, 6, 7, 2, 3, 0, 1))
        if it < OUTER - 1:
            for s in range(n_t):
                for b in range(blocks):
                    e = recv_flux[it, s, b * kp + species:(b + 1) * kp, :]
                    ends_own[s * blocks + b] = e
                    ends_all[(v * n_t + s) * blocks + b] = e
            for d in range(1, n_v):
                ends_copy(d).start()
        halo_recv(s_set)
        fill(s_set, ext_s)
        fields = (field_a, field_b)
        for n in range(SWEEPS):
            sweep(fields[n % 2], fields[(n + 1) % 2], n + 1, 3 * cz - 1 - n, n == SWEEPS - 1)
        final = fields[SWEEPS % 2]
        if it < OUTER - 1:
            for z in range(cz):
                for k in range(species):
                    own[3, z, k] = final[0, cz + z, k]
            make_pack(3)
        else:
            for z in range(cz):
                for k in range(species):
                    tissue_out[k, z] = final[0, cz + z, k]

    for d in range(1, n_t):
        a2a(send_vox, recv_vox, vox_ss, vox_rs, d).wait_send()
        for it in range(OUTER):
            a2a(send_val.at[it], recv_val.at[it], val_ss.at[it], val_rs.at[it], d).wait_send()
            a2a(send_flux.at[it], recv_flux.at[it], flux_ss.at[it], flux_rs.at[it], d).wait_send()
    for d in range(1, n_v):
        ends_copy(d).wait_send()
    for which in range(5):
        halo_done(which)


def solution(mesh):
    n_v, n_t = mesh.shape["vessel"], mesh.shape["tissue"]

    def shards(tissue, cons, inlet, flow, perm, count, seg, vox, weight, up):
        species, cz, cy, nx = tissue.shape
        blocks, _, slots = seg.shape
        kp, rows, pairs = species + 1, cz * cy, cz // 2
        vmem = pl.BlockSpec(memory_space=pltpu.VMEM)
        dma = pltpu.SemaphoreType.DMA
        tile = (species, cy, nx)
        message = pltpu.VMEM((OUTER, n_t, blocks * kp, slots), F32)
        ext = pltpu.VMEM((2, 3 * cz) + tile, F32)
        return pl.pallas_call(
            functools.partial(kernel, n_v, n_t),
            out_shape=(
                pltpu.VMEM(tissue.shape, F32),
                pltpu.VMEM((species, blocks, flow.shape[1]), F32),
            ),
            in_specs=[pl.BlockSpec(memory_space=pl.ANY)] * 10,
            out_specs=(vmem, vmem),
            scratch_shapes=[
                pltpu.VMEM(tissue.shape, F32), pltpu.VMEM(cons.shape, F32), pltpu.SMEM(inlet.shape, F32),
                pltpu.VMEM(flow.shape, F32), pltpu.SMEM(perm.shape, F32), pltpu.SMEM(count.shape, jnp.int32),
                pltpu.VMEM(seg.shape, jnp.int32), pltpu.VMEM(vox.shape, jnp.int32), pltpu.VMEM(weight.shape, F32),
                pltpu.SMEM(up.shape, jnp.int32), dma((10,)),
                pltpu.VMEM((n_t, blocks, slots), jnp.int32),
                pltpu.VMEM((n_t, blocks, slots), jnp.int32),
                pltpu.VMEM((n_t, LANES, blocks * slots), BF16),
                pltpu.VMEM((blocks, LANES, n_t * slots), BF16),
                pltpu.VMEM((2 * species * rows, nx), BF16),
                pltpu.VMEM((2 * species * rows, nx), F32),
                message, message, message, message,
                pltpu.VMEM((blocks, 1, n_t * slots), F32),
                pltpu.VMEM((blocks, 1, n_t * slots), F32),
                pltpu.VMEM((9, blocks * 2 * kp, LANES), F32),
                pltpu.VMEM((n_t * blocks, 1, slots), F32),
                pltpu.VMEM((n_v * n_t * blocks, 1, slots), F32),
                pltpu.VMEM((5, cz) + tile, F32),
                pltpu.VMEM((5, 2, pairs) + tile, F32),
                pltpu.VMEM((5, 2, cz) + tile, F32),
                pltpu.VMEM((5, 6, pairs) + tile, F32),
                ext, ext, ext, ext,
                pltpu.VMEM((2, 3 * cz, cy, nx), F32),
                dma((n_t,)), dma((n_t,)),
                dma((OUTER, n_t)), dma((OUTER, n_t)),
                dma((OUTER, n_t)), dma((OUTER, n_t)),
                dma((n_v,)), dma((n_v,)),
                dma((5, len(DIRS))), dma((5, len(DIRS))),
            ],
            compiler_params=pltpu.CompilerParams(collective_id=0, has_side_effects=True),
        )(tissue, cons, inlet, flow, perm, count, seg, vox, weight, up)

    both = ("vessel", "tissue")
    grid = P(None, "vessel", "tissue", None)
    return jax.shard_map(
        shards,
        mesh=mesh,
        in_specs=(
            grid, grid, P(None, both), P(both, None), P(), P(both, None),
            P(both, None, None), P(both, None, None), P(both, None, None), P(both),
        ),
        out_specs=(grid, P(None, both, None)),
        check_vma=False,
    )
```
